32 devices in a mesh: gx: 4 (over y, x), gy: 8 (over z, core).
Axes of the slice: x: 2, y: 2, z: 4, core: 2. Of those that a mesh axis runs over, the one named last changes fastest.
Arguments:
- height: float32 [1, 2048, 4096], P(None, 'gy', 'gx'), may hold values from -12 to 12
- zonal_velocity: float32 [1, 2048, 4096], P(None, 'gy', 'gx'), may hold values from -4 to 4
- meridional_velocity: float32 [1, 2048, 4096], P(None, 'gy', 'gx'), may hold values from -4 to 4
- wave_courant: float32 [1], replicated, may hold values from 4 to 24
Outputs:
- solution: float32 [1, 2048, 4096], P(None, 'gy', 'gx')
- new_zonal: float32 [1, 2048, 4096], P(None, 'gy', 'gx')
- new_meridional: float32 [1, 2048, 4096], P(None, 'gy', 'gx')
The draws below stay inside these ranges and needn't reach their ends.
All inputs are finite; a program needn't handle non-finite values.
Results may differ from the reference program's by a relative error of at most 0.0003.
Values sent between devices are 32-bit elements; how exact they have to be, the bound alone decides.
A program may use at most 64 MiB of HBM per device.

```python
import math
import jax
import jax.numpy as jnp

MODES = 1
ITERS = 3
NR = 2048
NC = 4096


def ramp_field(row_factor, col_factor):
    row_position = jnp.arange(NR, dtype=jnp.float32) / NR
    col_position = jnp.arange(NC, dtype=jnp.float32) / NC
    row_part = jnp.exp(row_position * jnp.log(row_factor)).reshape(1, NR, 1)
    col_part = jnp.exp(col_position * jnp.log(col_factor)).reshape(1, 1, NC)
    return row_part * col_part


def draw_height(key, part):
    key_noise = jax.random.fold_in(jax.random.fold_in(key, 17), 0)
    base_noise = jnp.clip(jax.random.normal(key_noise, (MODES, NR, NC), jnp.float32), -4.0, 4.0)
    samples = base_noise * ramp_field(jnp.sqrt(3.0), jnp.sqrt(3.0))
    return samples


def velocity_draw(key, salt):
    key_noise = jax.random.fold_in(key, salt)
    base_noise = jnp.clip(jax.random.normal(key_noise, (MODES, NR, NC), jnp.float32), -2.3, 2.3)
    samples = base_noise * ramp_field(jnp.sqrt(3.0), jnp.sqrt(3.0)) / jnp.sqrt(3.0)
    return samples


def draw_zonal_velocity(key, part):
    return velocity_draw(key, 29)


def draw_meridional_velocity(key, part):
    return velocity_draw(key, 41)


def setup_inputs(seed: int = 0) -> dict:
    key_of = jax.random.split(jax.random.key(seed), 5)
    height = draw_height(jax.random.fold_in(key_of[4], 71), 0)
    zonal_velocity = draw_zonal_velocity(jax.random.fold_in(key_of[4], 71), 0)
    meridional_velocity = draw_meridional_velocity(jax.random.fold_in(key_of[4], 71), 0)
    wave_courant = jnp.clip(jnp.exp(jax.random.uniform(key_of[3], (MODES,), jnp.float32, math.log(4.0), math.log(24.0))), 4.0, 24.0)
    return {"height": height, "zonal_velocity": zonal_velocity, "meridional_velocity": meridional_velocity, "wave_courant": wave_courant}


advect_courant = 0.2
implicit_weight = 0.25
explicit_weight = 0.5


def centered(values, axis):
    return 0.5 * (jnp.roll(values, -1, axis) - jnp.roll(values, 1, axis))


def upwind(values, speed, axis):
    backward = values - jnp.roll(values, 1, axis)
    forward = jnp.roll(values, -1, axis) - values
    return speed * jnp.where(speed > 0, backward, forward)


def advection(values, zonal, meridional):
    return -(upwind(values, zonal, 2) + upwind(values, meridional, 1))


def helmholtz(values, stiffness):
    second = (jnp.roll(values, -2, 2) + jnp.roll(values, 2, 2) + jnp.roll(values, -2, 1) + jnp.roll(values, 2, 1) - 4.0 * values) * 0.25
    return values - stiffness * second


def chebyshev(residual, stiffness):
    upper = 1.0 + 2.0 * stiffness
    center = (upper + 1.0) * 0.5
    half_width = (upper - 1.0) * 0.5
    ratio = center / half_width
    rho_prev = 1.0 / ratio
    update = residual / center
    approx = update
    for sweep_index in range(3):
        misfit = residual - helmholtz(approx, stiffness)
        rho_next = 1.0 / (2.0 * ratio - rho_prev)
        update = rho_next * rho_prev * update + (2.0 * rho_next / half_width) * misfit
        approx = approx + update
        rho_prev = rho_next
    return approx


def layer_sum(values):
    return jnp.sum(values, axis=(1, 2), keepdims=True)


def reference(height, zonal_velocity, meridional_velocity, wave_courant):
    wave_factor = (implicit_weight * wave_courant).reshape(-1, 1, 1)
    factor = explicit_weight * advect_courant
    section_height = height + factor * advection(height, zonal_velocity, meridional_velocity) - wave_factor * (centered(zonal_velocity, 2) + centered(meridional_velocity, 1))
    section_zonal = zonal_velocity + factor * advection(zonal_velocity, zonal_velocity, meridional_velocity) - wave_factor * centered(height, 2)
    section_meridional = meridional_velocity + factor * advection(meridional_velocity, zonal_velocity, meridional_velocity) - wave_factor * centered(height, 1)
    source = section_height - wave_factor * (centered(section_zonal, 2) + centered(section_meridional, 1))
    stiffness = wave_factor * wave_factor
    solution = jnp.zeros_like(source)
    residual = source
    precond = chebyshev(residual, stiffness)
    direction = precond
    precond_norm = layer_sum(residual * precond)
    for iteration in range(ITERS):
        product = helmholtz(direction, stiffness)
        step_length = precond_norm / layer_sum(direction * product)
        solution = solution + step_length * direction
        residual = residual - step_length * product
        if iteration + 1 < ITERS:
            precond = chebyshev(residual, stiffness)
            norm_next = layer_sum(residual * precond)
            direction = precond + (norm_next / precond_norm) * direction
            precond_norm = norm_next
    new_zonal = section_zonal - wave_factor * centered(solution, 2)
    new_meridional = section_meridional - wave_factor * centered(solution, 1)
    return solution, new_zonal, new_meridional
```

```python
import functools

import jax
import jax.numpy as jnp
from jax import lax
from jax.experimental import pallas as pl
from jax.experimental.pallas import tpu as pltpu
from jax.sharding import PartitionSpec as P

HALO = 32
LANES = 128
SUB = 8
MESH = pl.DeviceIdType.MESH

advect_courant = 0.2
implicit_weight = 0.25
explicit_weight = 0.5


def preconditioner_polynomial(stiff):
    one = jnp.ones_like(stiff)
    upper = 1.0 + 2.0 * stiff
    center = (upper + 1.0) * 0.5
    half = (upper - 1.0) * 0.5
    ratio = center / half
    sigma = stiff * 0.25
    rho = 1.0 / ratio
    update = [1.0 / center]
    approx = list(update)
    for _ in range(3):
        misfit = [one] + [jnp.zeros_like(stiff)] * len(approx)
        for k, value in enumerate(approx):
            misfit[k] = misfit[k] - center * value
            misfit[k + 1] = misfit[k + 1] + sigma * value
        rho_next = 1.0 / (2.0 * ratio - rho)
        first = rho_next * rho
        second = 2.0 * rho_next / half
        update = [
            (first * update[k] if k < len(update) else 0.0) + second * misfit[k]
            for k in range(len(misfit))
        ]
        approx = [
            (approx[k] if k < len(approx) else 0.0) + update[k] for k in range(len(update))
        ]
        rho = rho_next
    return approx, center, sigma


def kernel(
    nx, ny, rows, tiles,
    wave_ref, h_in, u_in, v_in, x_out, u_out, v_out,
    fields, su, sv, src, tmp_a, tmp_b, z0, q0, m0, n0, m1, n1,
    row_halo, pack, pack_halo, stage,
    red_send, red_gy, red_gx,
    load_sem, row_ss, row_rs, col_ss, col_rs,
    gy_ss, gy_rs, gx_ss, gx_rs, out_sem,
):
    gx = lax.axis_index("gx")
    gy = lax.axis_index("gy")
    right, left = lax.rem(gx + 1, nx), lax.rem(gx + nx - 1, nx)
    high, low = lax.rem(gy + 1, ny), lax.rem(gy + ny - 1, ny)
    width = tiles * LANES
    ring = tiles + 1
    inputs = (h_in, u_in, v_in)

    barrier = pltpu.get_barrier_semaphore()
    greeted = [{"gy": lax.rem(gy + o, ny)} for o in range(1, ny)]
    greeted += [{"gx": lax.rem(gx + o, nx)} for o in range(1, nx)]
    greeted += [{"gx": a, "gy": b} for a in (left, right) for b in (low, high)]
    for device in greeted:
        pl.semaphore_signal(barrier, inc=1, device_id=device, device_id_type=MESH)

    loads = {}
    for c in [0, tiles - 1] + list(range(1, tiles - 1)):
        for f in range(3):
            loads[f, c] = pltpu.make_async_copy(
                inputs[f].at[0, :, pl.ds(c * LANES, LANES)],
                fields.at[f, c, pl.ds(HALO, rows), :],
                load_sem.at[f, c],
            )
            loads[f, c].start()
    pl.semaphore_wait(barrier, len(greeted))

    row_copies = []
    for f in range(3):
        for side, device, first in ((0, high, rows - HALO), (1, low, 0)):
            row_copies.append(
                pltpu.make_async_remote_copy(
                    src_ref=inputs[f].at[0, pl.ds(first, HALO), :],
                    dst_ref=row_halo.at[side, f],
                    send_sem=row_ss.at[side, f],
                    recv_sem=row_rs.at[side, f],
                    device_id={"gy": device},
                    device_id_type=MESH,
                )
            )
            row_copies[-1].start()

    lane = lax.broadcasted_iota(jnp.int32, (SUB, LANES), 1)

    for f in range(3):
        loads[f, 0].wait()
        loads[f, tiles - 1].wait()
    for f in range(3):
        def pack_group(g, carry, f=f):
            for side, tile, at in ((0, tiles - 1, LANES - HALO), (1, 0, 0)):
                packed = None
                for j in range(4):
                    start = pl.multiple_of(HALO + g * 32 + j * SUB, SUB)
                    value = fields[f, tile, pl.ds(start, SUB), :]
                    shift = (j * 32 - at) % LANES
                    if shift:
                        value = pltpu.roll(value, shift, 1)
                    packed = value if packed is None else jnp.where(lane < j * 32, packed, value)
                pack[side, f, pl.ds(pl.multiple_of(g * SUB, SUB), SUB), :] = packed
            return carry

        lax.fori_loop(0, rows // 32, pack_group, 0)
    deep = rows // 4
    col_copies = []
    for side, device in ((0, right), (1, left)):
        for part, target, first, size, dest in (
            (0, {"gx": device}, 0, deep, SUB),
            (1, {"gx": device, "gy": high}, deep - SUB, SUB, 0),
            (2, {"gx": device, "gy": low}, 0, SUB, deep + SUB),
        ):
            col_copies.append(
                pltpu.make_async_remote_copy(
                    src_ref=pack.at[side, :, pl.ds(first, size), :],
                    dst_ref=pack_halo.at[side, :, pl.ds(dest, size), :],
                    send_sem=col_ss.at[side, part],
                    recv_sem=col_rs.at[side, part],
                    device_id=target,
                    device_id_type=MESH,
                )
            )
            col_copies[-1].start()

    wave = jnp.full((SUB, LANES), wave_ref[0], jnp.float32) * implicit_weight
    stiff = wave * wave
    coef, center, sigma = preconditioner_polynomial(stiff)

    for c in range(1, tiles - 1):
        for f in range(3):
            loads[f, c].wait()
    for copy in row_copies:
        copy.wait()
    for f in range(3):
        for c in range(tiles):
            cols = pl.ds(c * LANES, LANES)
            fields[f, c, pl.ds(0, HALO), :] = row_halo[0, f, :, cols]
            fields[f, c, pl.ds(HALO + rows, HALO), :] = row_halo[1, f, :, cols]
    for copy in col_copies:
        copy.wait()
    for f in range(3):
        def unpack_group(g, carry, f=f):
            at = pl.ds(pl.multiple_of(g * SUB, SUB), SUB)
            from_left = pack_halo[0, f, at, :]
            from_right = pack_halo[1, f, at, :]
            for j in range(4):
                shift_r = (-j * 32) % LANES
                shift_l = (LANES - HALO - j * 32) % LANES
                a = pltpu.roll(from_right, shift_r, 1) if shift_r else from_right
                b = pltpu.roll(from_left, shift_l, 1) if shift_l else from_left
                start = pl.multiple_of(g * 32 + j * SUB, SUB)
                fields[f, tiles, pl.ds(start, SUB), :] = jnp.where(lane < 64, a, b)
            return carry

        lax.fori_loop(0, (rows + 2 * HALO) // 32, unpack_group, 0)

    def lane_pairs(values, distance):
        to_right = [pltpu.roll(v, distance, 1) for v in values]
        to_left = [pltpu.roll(v, LANES - distance, 1) for v in values]
        from_left = [
            jnp.where(lane < distance, to_right[c - 1], to_right[c]) for c in range(len(values))
        ]
        from_right = [
            jnp.where(lane >= LANES - distance, to_left[(c + 1) % len(values)], to_left[c])
            for c in range(len(values))
        ]
        return from_left, from_right

    factor = explicit_weight * advect_courant
    half_wave = 0.5 * wave

    def section(i, carry):
        base = pl.multiple_of(i * SUB, SUB)
        at, up, down = (pl.ds(base + k, SUB) for k in (7, 6, 8))
        h = [fields[0, c, at, :] for c in range(ring)]
        u = [fields[1, c, at, :] for c in range(ring)]
        v = [fields[2, c, at, :] for c in range(ring)]
        sides = [lane_pairs(q, 1) for q in (h, u, v)]
        for c in range(ring):
            east = u[c] > 0
            north = v[c] > 0
            fu = factor * u[c]
            fv = factor * v[c]
            moved = []
            grads = []
            for f, q in enumerate((h, u, v)):
                w, e = sides[f][0][c], sides[f][1][c]
                s, n = fields[f, c, up, :], fields[f, c, down, :]
                mid = q[c]
                moved.append(
                    mid
                    - (
                        fu * jnp.where(east, mid - w, e - mid)
                        + fv * jnp.where(north, mid - s, n - mid)
                    )
                )
                grads.append((e - w, n - s))
            src[c, at, :] = moved[0] - half_wave * (grads[1][0] + grads[2][1])
            su[c, at, :] = moved[1] - half_wave * grads[0][0]
            sv[c, at, :] = moved[2] - half_wave * grads[0][1]
        return carry

    lax.fori_loop(0, (rows + 2 * HALO) // SUB - 1, section, 0)

    def source(i, carry):
        base = pl.multiple_of(i * SUB, SUB)
        at, up, down = (pl.ds(base + k, SUB) for k in (0, -1, 1))
        w, e = lane_pairs([su[c, at, :] for c in range(ring)], 1)
        for c in range(ring):
            grad = (e[c] - w[c]) + (sv[c, down, :] - sv[c, up, :])
            src[c, at, :] = src[c, at, :] - half_wave * grad
        return carry

    lax.fori_loop(1, (rows + 2 * HALO) // SUB - 1, source, 0)

    def neighbour_sums(ref, base):
        mids = [ref[c, pl.ds(base, SUB), :] for c in range(ring)]
        w, e = lane_pairs(mids, 2)
        sums = [
            (w[c] + e[c]) + (ref[c, pl.ds(base - 2, SUB), :] + ref[c, pl.ds(base + 2, SUB), :])
            for c in range(ring)
        ]
        return mids, sums

    def stencil(step, ref, out, combine):
        valid = 24 - 2 * step
        lo = (HALO - valid) // SUB
        hi = -(-(HALO + rows + valid) // SUB)

        def body(i, carry):
            base = pl.multiple_of(i * SUB, SUB)
            mids, sums = neighbour_sums(ref, base)
            for c in range(ring):
                out[c, pl.ds(base, SUB), :] = combine(c, base, mids[c], sums[c])
            return carry

        lax.fori_loop(lo, hi, body, 0)

    def precondition_half(step, r, z, first):
        at = lambda c, base: r[c, pl.ds(base, SUB), :]
        if first:
            stencil(step, r, tmp_a, lambda c, b, mid, s: coef[2] * mid + coef[3] * s)
            stencil(step + 1, tmp_a, tmp_b, lambda c, b, mid, s: coef[1] * at(c, b) + s)
        else:
            stencil(step, tmp_b, z, lambda c, b, mid, s: coef[0] * at(c, b) + s)

    def operator(step, z, q):
        stencil(step, z, q, lambda c, b, mid, s: center * mid - sigma * s)

    def dots(index, load):
        def body(i, carry):
            first, second = carry
            base = pl.multiple_of(HALO + i * SUB, SUB)
            for c in range(tiles):
                r, z, w = load(lambda ref: ref[c, pl.ds(base, SUB), :])
                first[c % 2] = first[c % 2] + r * z
                second[c % 2] = second[c % 2] + z * w
            return first, second

        zero = jnp.zeros((SUB, LANES), jnp.float32)
        first, second = lax.fori_loop(
            0, rows // SUB, body, ([zero, zero], [zero, zero])
        )
        red_send[index, 0, pl.ds(0, 1), :] = jnp.sum(first[0] + first[1], axis=0, keepdims=True)
        red_send[index, 0, pl.ds(1, 1), :] = jnp.sum(second[0] + second[1], axis=0, keepdims=True)

    def gather(index, phase):
        count, axis, me = ((ny, "gy", gy), (nx, "gx", gx))[phase]
        slots, ss, rs = ((red_gy, gy_ss, gy_rs), (red_gx, gx_ss, gx_rs))[phase]
        copies = []
        for o in range(1, count):
            copies.append(
                pltpu.make_async_remote_copy(
                    src_ref=red_send.at[index, phase],
                    dst_ref=slots.at[index, o],
                    send_sem=ss.at[index, o],
                    recv_sem=rs.at[index, o],
                    device_id={axis: lax.rem(me + o, count)},
                    device_id_type=MESH,
                )
            )
            copies[-1].start()
        return copies

    def gathered(index, phase, copies):
        slots = (red_gy, red_gx)[phase]
        for copy in copies:
            copy.wait()
        total = red_send[index, phase]
        for o in range(1, len(copies) + 1):
            total = total + slots[index, o]
        return total

    def totals(index, copies):
        total = gathered(index, 1, copies)
        sums = jnp.sum(total, axis=1, keepdims=True)
        full = jnp.broadcast_to(sums, (SUB, LANES))
        return (
            jnp.broadcast_to(full[0:1, :], (SUB, LANES)),
            jnp.broadcast_to(full[1:2, :], (SUB, LANES)),
        )

    def first_phase(index, load):
        red_send[index, 0] = jnp.zeros((SUB, LANES), jnp.float32)
        dots(index, load)
        return gather(index, 0)

    def second_phase(index, copies):
        red_send[index, 1] = gathered(index, 0, copies)
        return gather(index, 1)

    precondition_half(1, src, z0, True)
    precondition_half(3, src, z0, False)
    operator(4, z0, q0)
    copies = first_phase(0, lambda get: (get(src), get(z0), get(q0)))
    precondition_half(5, q0, m0, True)
    copies = second_phase(0, copies)
    precondition_half(7, q0, m0, False)
    operator(8, m0, n0)
    rz0, zw0 = totals(0, copies)
    alpha0 = rz0 / zw0

    copies = first_phase(
        1,
        lambda get: (
            get(src) - alpha0 * get(q0),
            get(z0) - alpha0 * get(m0),
            get(q0) - alpha0 * get(n0),
        ),
    )
    precondition_half(9, n0, m1, True)
    copies = second_phase(1, copies)
    precondition_half(11, n0, m1, False)
    operator(12, m1, n1)
    rz1, zw1 = totals(1, copies)
    beta1 = rz1 / rz0
    alpha1 = rz1 / (zw1 - beta1 * rz1 / alpha0)

    linear = alpha0 + alpha1 * (1.0 + beta1)
    square = alpha0 * alpha1
    copies = first_phase(
        2,
        lambda get: (
            get(src) - linear * get(q0) + square * get(n0),
            get(z0) - linear * get(m0) + square * get(m1),
            get(q0) - linear * get(n0) + square * get(n1),
        ),
    )
    copies = second_phase(2, copies)
    rz2, zw2 = totals(2, copies)
    beta2 = rz2 / rz1
    alpha2 = rz2 / (zw2 - beta2 * rz2 / alpha1)

    along = alpha1 + alpha2 * beta2
    take_z0 = alpha0 + along * (1.0 + beta1) + alpha2
    take_m0 = -(along * alpha0 + alpha2 * linear)
    take_m1 = alpha2 * square

    solved = tmp_a

    def combine(i, carry):
        base = pl.multiple_of(i * SUB, SUB)
        at = pl.ds(base, SUB)
        for c in range(ring):
            solved[c, at, :] = take_z0 * z0[c, at, :] + take_m0 * m0[c, at, :] + take_m1 * m1[c, at, :]
        return carry

    lax.fori_loop(HALO // SUB - 1, (HALO + rows) // SUB + 1, combine, 0)

    outputs = (x_out, u_out, v_out)
    chunks = 4
    chunk = rows // chunks
    writes = []
    for k in range(chunks):
        def finish(i, carry, k=k):
            base = pl.multiple_of(HALO + k * chunk + i * SUB, SUB)
            to = pl.ds(pl.multiple_of(k * chunk + i * SUB, SUB), SUB)
            mids = [solved[c, pl.ds(base, SUB), :] for c in range(ring)]
            w, e = lane_pairs(mids, 1)
            for c in range(tiles):
                at = pl.ds(base, SUB)
                cols = pl.ds(c * LANES, LANES)
                north = solved[c, pl.ds(base + 1, SUB), :]
                south = solved[c, pl.ds(base - 1, SUB), :]
                stage[0, to, cols] = mids[c]
                stage[1, to, cols] = su[c, at, :] - half_wave * (e[c] - w[c])
                stage[2, to, cols] = sv[c, at, :] - half_wave * (north - south)
            return carry

        lax.fori_loop(0, chunk // SUB, finish, 0)
        for f in range(3):
            part = pl.ds(k * chunk, chunk)
            writes.append(
                pltpu.make_async_copy(
                    stage.at[f, part, :], outputs[f].at[0, part, :], out_sem.at[f, k]
                )
            )
            writes[-1].start()
    for copy in writes:
        copy.wait()


def local(mesh, height, zonal_velocity, meridional_velocity, wave_courant):
    nx, ny = mesh.shape["gx"], mesh.shape["gy"]
    _, rows, width = height.shape
    tiles = width // LANES
    extended = (tiles + 1, rows + 2 * HALO, LANES)
    f32 = jnp.float32
    dma = pltpu.SemaphoreType.DMA
    hbm = pl.BlockSpec(memory_space=pl.ANY)
    out = jax.ShapeDtypeStruct(height.shape, f32)
    return pl.pallas_call(
        functools.partial(kernel, nx, ny, rows, tiles),
        out_shape=(out, out, out),
        in_specs=[pl.BlockSpec(memory_space=pltpu.SMEM), hbm, hbm, hbm],
        out_specs=(hbm, hbm, hbm),
        scratch_shapes=[pltpu.VMEM((3,) + extended, f32)]
        + [pltpu.VMEM(extended, f32)] * 11
        + [
            pltpu.VMEM((2, 3, HALO, width), f32),
            pltpu.VMEM((2, 3, rows // 4, LANES), f32),
            pltpu.VMEM((2, 3, rows // 4 + 2 * SUB, LANES), f32),
            pltpu.VMEM((3, rows, width), f32),
            pltpu.VMEM((3, 2, SUB, LANES), f32),
            pltpu.VMEM((3, ny, SUB, LANES), f32),
            pltpu.VMEM((3, nx, SUB, LANES), f32),
            dma((3, tiles)),
            dma((2, 3)),
            dma((2, 3)),
            dma((2, 3)),
            dma((2, 3)),
            dma((3, ny)),
            dma((3, ny)),
            dma((3, nx)),
            dma((3, nx)),
            dma((3, 4)),
        ],
        compiler_params=pltpu.CompilerParams(
            collective_id=0, has_side_effects=True, vmem_limit_bytes=56 * 1024 * 1024
        ),
    )(wave_courant, height, zonal_velocity, meridional_velocity)


def solution(mesh):
    spec = P(None, "gy", "gx")
    return jax.shard_map(
        functools.partial(local, mesh),
        mesh=mesh,
        in_specs=(spec, spec, spec, P()),
        out_specs=(spec, spec, spec),
        check_vma=False,
    )
```

```python
import functools

import jax
import jax.numpy as jnp
from jax import lax
from jax.experimental import pallas as pl
from jax.experimental.pallas import tpu as pltpu
from jax.sharding import PartitionSpec as P

HALO = 32
LANES = 128
SUB = 8
MESH = pl.DeviceIdType.MESH

advect_courant = 0.2
implicit_weight = 0.25
explicit_weight = 0.5


def preconditioner_polynomial(stiff):
    one = jnp.ones_like(stiff)
    upper = 1.0 + 2.0 * stiff
    center = (upper + 1.0) * 0.5
    half = (upper - 1.0) * 0.5
    ratio = center / half
    sigma = stiff * 0.25
    rho = 1.0 / ratio
    update = [1.0 / center]
    approx = list(update)
    for _ in range(3):
        misfit = [one] + [jnp.zeros_like(stiff)] * len(approx)
        for k, value in enumerate(approx):
            misfit[k] = misfit[k] - center * value
            misfit[k + 1] = misfit[k + 1] + sigma * value
        rho_next = 1.0 / (2.0 * ratio - rho)
        first = rho_next * rho
        second = 2.0 * rho_next / half
        update = [
            (first * update[k] if k < len(update) else 0.0) + second * misfit[k]
            for k in range(len(misfit))
        ]
        approx = [
            (approx[k] if k < len(approx) else 0.0) + update[k] for k in range(len(update))
        ]
        rho = rho_next
    return approx, center, sigma


def kernel(
    nx, ny, rows, tiles,
    wave_ref, h_in, u_in, v_in, x_out, u_out, v_out,
    fields, su, sv, src, tmp_a, tmp_b, z0, q0, m0, n0, m1, n1,
    row_halo, pack, pack_halo, stage,
    red_send, red_gy, red_gx,
    load_sem, row_ss, row_rs, col_ss, col_rs,
    gy_ss, gy_rs, gx_ss, gx_rs, out_sem,
):
    gx = lax.axis_index("gx")
    gy = lax.axis_index("gy")
    right, left = lax.rem(gx + 1, nx), lax.rem(gx + nx - 1, nx)
    high, low = lax.rem(gy + 1, ny), lax.rem(gy + ny - 1, ny)
    width = tiles * LANES
    ring = tiles + 1
    inputs = (h_in, u_in, v_in)

    barrier = pltpu.get_barrier_semaphore()
    greeted = [{"gy": lax.rem(gy + o, ny)} for o in range(1, ny)]
    greeted += [{"gx": lax.rem(gx + o, nx)} for o in range(1, nx)]
    greeted += [{"gx": a, "gy": b} for a in (left, right) for b in (low, high)]
    for device in greeted:
        pl.semaphore_signal(barrier, inc=1, device_id=device, device_id_type=MESH)

    loads = {}
    for c in [0, tiles - 1] + list(range(1, tiles - 1)):
        for f in range(3):
            loads[f, c] = pltpu.make_async_copy(
                inputs[f].at[0, :, pl.ds(c * LANES, LANES)],
                fields.at[f, c, pl.ds(HALO, rows), :],
                load_sem.at[f, c],
            )
            loads[f, c].start()
    pl.semaphore_wait(barrier, len(greeted))

    row_copies = []
    for f in range(3):
        for side, device, first in ((0, high, rows - HALO), (1, low, 0)):
            row_copies.append(
                pltpu.make_async_remote_copy(
                    src_ref=inputs[f].at[0, pl.ds(first, HALO), :],
                    dst_ref=row_halo.at[side, f],
                    send_sem=row_ss.at[side, f],
                    recv_sem=row_rs.at[side, f],
                    device_id={"gy": device},
                    device_id_type=MESH,
                )
            )
            row_copies[-1].start()

    lane = lax.broadcasted_iota(jnp.int32, (SUB, LANES), 1)

    for f in range(3):
        loads[f, 0].wait()
        loads[f, tiles - 1].wait()
    for f in range(3):
        def pack_group(g, carry, f=f):
            for side, tile, at in ((0, tiles - 1, LANES - HALO), (1, 0, 0)):
                packed = None
                for j in range(4):
                    start = pl.multiple_of(HALO + g * 32 + j * SUB, SUB)
                    value = fields[f, tile, pl.ds(start, SUB), :]
                    shift = (j * 32 - at) % LANES
                    if shift:
                        value = pltpu.roll(value, shift, 1)
                    packed = value if packed is None else jnp.where(lane < j * 32, packed, value)
                pack[side, f, pl.ds(pl.multiple_of(g * SUB, SUB), SUB), :] = packed
            return carry

        lax.fori_loop(0, rows // 32, pack_group, 0, unroll=4)
    deep = rows // 4
    col_copies = []
    for side, device in ((0, right), (1, left)):
        for part, target, first, size, dest in (
            (0, {"gx": device}, 0, deep, SUB),
            (1, {"gx": device, "gy": high}, deep - SUB, SUB, 0),
            (2, {"gx": device, "gy": low}, 0, SUB, deep + SUB),
        ):
            col_copies.append(
                pltpu.make_async_remote_copy(
                    src_ref=pack.at[side, :, pl.ds(first, size), :],
                    dst_ref=pack_halo.at[side, :, pl.ds(dest, size), :],
                    send_sem=col_ss.at[side, part],
                    recv_sem=col_rs.at[side, part],
                    device_id=target,
                    device_id_type=MESH,
                )
            )
            col_copies[-1].start()

    wave = jnp.full((SUB, LANES), wave_ref[0], jnp.float32) * implicit_weight
    stiff = wave * wave
    coef, center, sigma = preconditioner_polynomial(stiff)

    for c in range(1, tiles - 1):
        for f in range(3):
            loads[f, c].wait()
    def lane_pairs(values, distance):
        to_right = [pltpu.roll(v, distance, 1) for v in values]
        to_left = [pltpu.roll(v, LANES - distance, 1) for v in values]
        from_left = [
            jnp.where(lane < distance, to_right[c - 1], to_right[c]) for c in range(len(values))
        ]
        from_right = [
            jnp.where(lane >= LANES - distance, to_left[(c + 1) % len(values)], to_left[c])
            for c in range(len(values))
        ]
        return from_left, from_right

    factor = explicit_weight * advect_courant
    half_wave = 0.5 * wave

    def section(first, last, chosen, unroll):
        def body(i, carry):
            base = pl.multiple_of(i * SUB, SUB)
            at, up, down = (pl.ds(base + k, SUB) for k in (7, 6, 8))
            mids, to_right, to_left = {}, {}, {}

            def mid_of(f, c):
                if (f, c) not in mids:
                    mids[f, c] = fields[f, c, at, :]
                return mids[f, c]

            def shifted(f, c):
                before, after = (c - 1) % ring, (c + 1) % ring
                for k in (before, c):
                    if (f, k) not in to_right:
                        to_right[f, k] = pltpu.roll(mid_of(f, k), 1, 1)
                for k in (c, after):
                    if (f, k) not in to_left:
                        to_left[f, k] = pltpu.roll(mid_of(f, k), LANES - 1, 1)
                west = jnp.where(lane < 1, to_right[f, before], to_right[f, c])
                return west, jnp.where(lane >= LANES - 1, to_left[f, after], to_left[f, c])

            for c in chosen:
                u, v = mid_of(1, c), mid_of(2, c)
                east = u > 0
                north = v > 0
                fu = factor * u
                fv = factor * v
                moved = []
                grads = []
                for f in range(3):
                    w, e = shifted(f, c)
                    s, n = fields[f, c, up, :], fields[f, c, down, :]
                    mid = mid_of(f, c)
                    moved.append(
                        mid
                        - (
                            fu * jnp.where(east, mid - w, e - mid)
                            + fv * jnp.where(north, mid - s, n - mid)
                        )
                    )
                    grads.append((e - w, n - s))
                src[c, at, :] = moved[0] - half_wave * (grads[1][0] + grads[2][1])
                su[c, at, :] = moved[1] - half_wave * grads[0][0]
                sv[c, at, :] = moved[2] - half_wave * grads[0][1]
            return carry

        lax.fori_loop(first, last, body, 0, unroll=unroll)

    begin = HALO // SUB
    end = begin + rows // SUB - 1
    section(begin, end, range(1, tiles - 1), 4)
    for copy in col_copies:
        copy.wait()
    for f in range(3):
        def unpack_group(g, carry, f=f):
            at = pl.ds(pl.multiple_of(g * SUB, SUB), SUB)
            from_left = pack_halo[0, f, at, :]
            from_right = pack_halo[1, f, at, :]
            for j in range(4):
                shift_r = (-j * 32) % LANES
                shift_l = (LANES - HALO - j * 32) % LANES
                a = pltpu.roll(from_right, shift_r, 1) if shift_r else from_right
                b = pltpu.roll(from_left, shift_l, 1) if shift_l else from_left
                start = pl.multiple_of(g * 32 + j * SUB, SUB)
                fields[f, tiles, pl.ds(start, SUB), :] = jnp.where(lane < 64, a, b)
            return carry

        lax.fori_loop(0, (rows + 2 * HALO) // 32, unpack_group, 0, unroll=5)

    section(begin, end, (tiles - 1, tiles, 0), 4)
    for copy in row_copies:
        copy.wait()
    for f in range(3):
        for c in range(tiles):
            cols = pl.ds(c * LANES, LANES)
            fields[f, c, pl.ds(0, HALO), :] = row_halo[0, f, :, cols]
            fields[f, c, pl.ds(HALO + rows, HALO), :] = row_halo[1, f, :, cols]
    section(0, begin, range(ring), 4)
    section(end, end + begin, range(ring), 4)

    def source(i, carry):
        base = pl.multiple_of(i * SUB, SUB)
        at, up, down = (pl.ds(base + k, SUB) for k in (0, -1, 1))
        w, e = lane_pairs([su[c, at, :] for c in range(ring)], 1)
        for c in range(ring):
            grad = (e[c] - w[c]) + (sv[c, down, :] - sv[c, up, :])
            src[c, at, :] = src[c, at, :] - half_wave * grad
        return carry

    lax.fori_loop(1, (rows + 2 * HALO) // SUB - 1, source, 0, unroll=8)

    def neighbour_sums(ref, base):
        mids = [ref[c, pl.ds(base, SUB), :] for c in range(ring)]
        w, e = lane_pairs(mids, 2)
        sums = [
            (w[c] + e[c]) + (ref[c, pl.ds(base - 2, SUB), :] + ref[c, pl.ds(base + 2, SUB), :])
            for c in range(ring)
        ]
        return mids, sums

    def stencil(step, ref, out, combine):
        valid = 24 - 2 * step
        lo = (HALO - valid) // SUB
        hi = -(-(HALO + rows + valid) // SUB)

        def body(i, carry):
            base = pl.multiple_of(i * SUB, SUB)
            mids, sums = neighbour_sums(ref, base)
            for c in range(ring):
                out[c, pl.ds(base, SUB), :] = combine(c, base, mids[c], sums[c])
            return carry

        lax.fori_loop(lo, hi, body, 0, unroll=8)

    def precondition_half(step, r, z, first):
        at = lambda c, base: r[c, pl.ds(base, SUB), :]
        if first:
            stencil(step, r, tmp_a, lambda c, b, mid, s: coef[2] * mid + coef[3] * s)
            stencil(step + 1, tmp_a, tmp_b, lambda c, b, mid, s: coef[1] * at(c, b) + s)
        else:
            stencil(step, tmp_b, z, lambda c, b, mid, s: coef[0] * at(c, b) + s)

    def operator(step, z, q):
        stencil(step, z, q, lambda c, b, mid, s: center * mid - sigma * s)

    def dots(index, load):
        def body(i, carry):
            first, second = carry
            base = pl.multiple_of(HALO + i * SUB, SUB)
            for c in range(tiles):
                r, z, w = load(lambda ref: ref[c, pl.ds(base, SUB), :])
                first[c % 2] = first[c % 2] + r * z
                second[c % 2] = second[c % 2] + z * w
            return first, second

        zero = jnp.zeros((SUB, LANES), jnp.float32)
        first, second = lax.fori_loop(
            0, rows // SUB, body, ([zero, zero], [zero, zero]), unroll=8
        )
        red_send[index, 0, pl.ds(0, 1), :] = jnp.sum(first[0] + first[1], axis=0, keepdims=True)
        red_send[index, 0, pl.ds(1, 1), :] = jnp.sum(second[0] + second[1], axis=0, keepdims=True)

    def gather(index, phase):
        count, axis, me = ((ny, "gy", gy), (nx, "gx", gx))[phase]
        slots, ss, rs = ((red_gy, gy_ss, gy_rs), (red_gx, gx_ss, gx_rs))[phase]
        copies = []
        for o in range(1, count):
            copies.append(
                pltpu.make_async_remote_copy(
                    src_ref=red_send.at[index, phase],
                    dst_ref=slots.at[index, o],
                    send_sem=ss.at[index, o],
                    recv_sem=rs.at[index, o],
                    device_id={axis: lax.rem(me + o, count)},
                    device_id_type=MESH,
                )
            )
            copies[-1].start()
        return copies

    def gathered(index, phase, copies):
        slots = (red_gy, red_gx)[phase]
        for copy in copies:
            copy.wait()
        total = red_send[index, phase]
        for o in range(1, len(copies) + 1):
            total = total + slots[index, o]
        return total

    def totals(index, copies):
        total = gathered(index, 1, copies)
        sums = jnp.sum(total, axis=1, keepdims=True)
        full = jnp.broadcast_to(sums, (SUB, LANES))
        return (
            jnp.broadcast_to(full[0:1, :], (SUB, LANES)),
            jnp.broadcast_to(full[1:2, :], (SUB, LANES)),
        )

    def first_phase(index, load):
        red_send[index, 0] = jnp.zeros((SUB, LANES), jnp.float32)
        dots(index, load)
        return gather(index, 0)

    def second_phase(index, copies):
        red_send[index, 1] = gathered(index, 0, copies)
        return gather(index, 1)

    precondition_half(1, src, z0, True)
    precondition_half(3, src, z0, False)
    operator(4, z0, q0)
    copies = first_phase(0, lambda get: (get(src), get(z0), get(q0)))
    precondition_half(5, q0, m0, True)
    copies = second_phase(0, copies)
    precondition_half(7, q0, m0, False)
    operator(8, m0, n0)
    rz0, zw0 = totals(0, copies)
    alpha0 = rz0 / zw0

    copies = first_phase(
        1,
        lambda get: (
            get(src) - alpha0 * get(q0),
            get(z0) - alpha0 * get(m0),
            get(q0) - alpha0 * get(n0),
        ),
    )
    precondition_half(9, n0, m1, True)
    copies = second_phase(1, copies)
    precondition_half(11, n0, m1, False)
    operator(12, m1, n1)
    rz1, zw1 = totals(1, copies)
    beta1 = rz1 / rz0
    alpha1 = rz1 / (zw1 - beta1 * rz1 / alpha0)

    linear = alpha0 + alpha1 * (1.0 + beta1)
    square = alpha0 * alpha1
    copies = first_phase(
        2,
        lambda get: (
            get(src) - linear * get(q0) + square * get(n0),
            get(z0) - linear * get(m0) + square * get(m1),
            get(q0) - linear * get(n0) + square * get(n1),
        ),
    )
    copies = second_phase(2, copies)
    rz2, zw2 = totals(2, copies)
    beta2 = rz2 / rz1
    alpha2 = rz2 / (zw2 - beta2 * rz2 / alpha1)

    along = alpha1 + alpha2 * beta2
    take_z0 = alpha0 + along * (1.0 + beta1) + alpha2
    take_m0 = -(along * alpha0 + alpha2 * linear)
    take_m1 = alpha2 * square

    solved = tmp_a

    def combine(i, carry):
        base = pl.multiple_of(i * SUB, SUB)
        at = pl.ds(base, SUB)
        for c in range(ring):
            solved[c, at, :] = take_z0 * z0[c, at, :] + take_m0 * m0[c, at, :] + take_m1 * m1[c, at, :]
        return carry

    lax.fori_loop(HALO // SUB - 1, (HALO + rows) // SUB + 1, combine, 0, unroll=4)

    outputs = (x_out, u_out, v_out)
    chunks = 4
    chunk = rows // chunks
    writes = []
    for k in range(chunks):
        def finish(i, carry, k=k):
            base = pl.multiple_of(HALO + k * chunk + i * SUB, SUB)
            to = pl.ds(pl.multiple_of(k * chunk + i * SUB, SUB), SUB)
            mids = [solved[c, pl.ds(base, SUB), :] for c in range(ring)]
            w, e = lane_pairs(mids, 1)
            for c in range(tiles):
                at = pl.ds(base, SUB)
                cols = pl.ds(c * LANES, LANES)
                north = solved[c, pl.ds(base + 1, SUB), :]
                south = solved[c, pl.ds(base - 1, SUB), :]
                stage[0, to, cols] = mids[c]
                stage[1, to, cols] = su[c, at, :] - half_wave * (e[c] - w[c])
                stage[2, to, cols] = sv[c, at, :] - half_wave * (north - south)
            return carry

        lax.fori_loop(0, chunk // SUB, finish, 0, unroll=4)
        for f in range(3):
            part = pl.ds(k * chunk, chunk)
            writes.append(
                pltpu.make_async_copy(
                    stage.at[f, part, :], outputs[f].at[0, part, :], out_sem.at[f, k]
                )
            )
            writes[-1].start()
    for copy in writes:
        copy.wait()


def local(mesh, height, zonal_velocity, meridional_velocity, wave_courant):
    nx, ny = mesh.shape["gx"], mesh.shape["gy"]
    _, rows, width = height.shape
    tiles = width // LANES
    extended = (tiles + 1, rows + 2 * HALO, LANES)
    f32 = jnp.float32
    dma = pltpu.SemaphoreType.DMA
    hbm = pl.BlockSpec(memory_space=pl.ANY)
    out = jax.ShapeDtypeStruct(height.shape, f32)
    return pl.pallas_call(
        functools.partial(kernel, nx, ny, rows, tiles),
        out_shape=(out, out, out),
        in_specs=[pl.BlockSpec(memory_space=pltpu.SMEM), hbm, hbm, hbm],
        out_specs=(hbm, hbm, hbm),
        scratch_shapes=[pltpu.VMEM((3,) + extended, f32)]
        + [pltpu.VMEM(extended, f32)] * 11
        + [
            pltpu.VMEM((2, 3, HALO, width), f32),
            pltpu.VMEM((2, 3, rows // 4, LANES), f32),
            pltpu.VMEM((2, 3, rows // 4 + 2 * SUB, LANES), f32),
            pltpu.VMEM((3, rows, width), f32),
            pltpu.VMEM((3, 2, SUB, LANES), f32),
            pltpu.VMEM((3, ny, SUB, LANES), f32),
            pltpu.VMEM((3, nx, SUB, LANES), f32),
            dma((3, tiles)),
            dma((2, 3)),
            dma((2, 3)),
            dma((2, 3)),
            dma((2, 3)),
            dma((3, ny)),
            dma((3, ny)),
            dma((3, nx)),
            dma((3, nx)),
            dma((3, 4)),
        ],
        compiler_params=pltpu.CompilerParams(
            collective_id=0, has_side_effects=True, vmem_limit_bytes=56 * 1024 * 1024
        ),
    )(wave_courant, height, zonal_velocity, meridional_velocity)


def solution(mesh):
    spec = P(None, "gy", "gx")
    return jax.shard_map(
        functools.partial(local, mesh),
        mesh=mesh,
        in_specs=(spec, spec, spec, P()),
        out_specs=(spec, spec, spec),
        check_vma=False,
    )
```
